128 devices in a mesh: ctx: 32 (over x, z, core), fsdp: 4 (over y).
Axes of the slice: x: 4, y: 4, z: 4, core: 2. Of those that a mesh axis runs over, the one named last changes fastest.
Arguments:
- tokens: bfloat16 [4, 8192, 8192], P('fsdp', 'ctx'), may hold values from -6 to 6
- queries: bfloat16 [4, 8192, 8192], P('fsdp', 'ctx'), may hold values from -384 to 384
- kv_weight: bfloat16 [8192, 2048], P(None, 'fsdp'), may hold values from -0.0625 to 0.0625
- block_list: int32 [8, 64, 8], replicated, may hold values from 0 to 63, as said below
- counts: int32 [8, 64], replicated, may hold values from 4 to 8, as said below
Outputs:
- attended: bfloat16 [4, 8192, 8192], P('fsdp', 'ctx')
The draws below stay inside these ranges and needn't reach their ends.
Inputs may be any that keep to these rules, and one draw needn't show every extreme that they name: `block_list`: for each g and b the first counts[g, b] entries are distinct: block b, blocks b - 1 and b + 1 modulo 64 (the window wraps at the sequence's ends), the two global blocks of group g, and random blocks; the later entries are further distinct blocks. `counts`: some list has 8 live entries in every draw; loads differ from group to group.
All inputs are finite; a program needn't handle non-finite values.
Results may differ from the reference program's by a relative error of at most 0.007.
The reference program's roundings to bfloat16 on the way (of `keyvals` and `rounded`) count: a program that leaves them out, or rounds other values in their place, can miss the bound.
Values may be sent and summed in bfloat16 or wider, within the bound.
A program may use at most 192 MiB of HBM per device.

```python
import jax
import jax.numpy as jnp
from jax import lax

D = 8192
HQ = 64
KVH = 8
DH = 128
BLK = 128
RMOST = 3
MAXK = 8
SEQS = 4
LEN = 8192


def draw_queries(key, part):
    normal_part = jnp.clip(jax.random.normal(key, (SEQS, LEN, HQ, DH), jnp.float32), -6.0, 6.0)
    return normal_part.reshape(SEQS, LEN, HQ * DH).astype(jnp.bfloat16)


def block_plan(key):
    blocks = LEN // BLK
    plan_key = jax.random.fold_in(key, 101)
    order_key, global_key, cap_key, chosen_key, extra_key = jax.random.split(plan_key, 5)
    ranking = jax.vmap(lambda sub_key: jax.random.permutation(sub_key, blocks))(jax.random.split(order_key, KVH * blocks))
    ranking = ranking.reshape(KVH, blocks, blocks).astype(jnp.int32)
    global_rank = jax.vmap(lambda sub_key: jax.random.permutation(sub_key, blocks))(jax.random.split(global_key, KVH)).astype(jnp.int32)
    first_global = global_rank[:, 0]
    second_global = global_rank[:, 1]
    column = jnp.arange(blocks, dtype=jnp.int32)
    offset = (column[None, :] - column[:, None]) % blocks
    priority = ranking + 16
    priority = jnp.where(offset[None] == 0, 0, priority)
    priority = jnp.where(offset[None] == blocks - 1, 1, priority)
    priority = jnp.where(offset[None] == 1, 2, priority)
    is_first = column[None, None, :] == first_global[:, None, None]
    priority = jnp.where(is_first, jnp.minimum(priority, 3), priority)
    is_second = column[None, None, :] == second_global[:, None, None]
    priority = jnp.where(is_second, jnp.minimum(priority, 4), priority)
    ordering = jnp.argsort(priority, axis=2)
    picked = ordering[:, :, :MAXK].astype(jnp.int32)
    first_gap = (first_global[:, None] - column[None, :]) % blocks
    second_gap = (second_global[:, None] - column[None, :]) % blocks
    first_inside = ((first_gap == 0) | (first_gap == 1) | (first_gap == blocks - 1)).astype(jnp.int32)
    second_inside = ((second_gap == 0) | (second_gap == 1) | (second_gap == blocks - 1)).astype(jnp.int32)
    window_global = 5 - first_inside - second_inside
    group_ids = jnp.arange(KVH, dtype=jnp.int32)
    busiest = jax.random.randint(chosen_key, (), 0, KVH)
    caps = jax.random.randint(cap_key, (KVH,), 1, RMOST + 1)
    caps = jnp.where(group_ids == busiest, RMOST, caps)
    extra = jax.random.randint(extra_key, (KVH, blocks), 1, caps[:, None] + 1)
    extra = jnp.where(group_ids[:, None] == busiest, RMOST, extra)
    return (picked, (window_global + extra).astype(jnp.int32))


def draw_block_list(key, part):
    return block_plan(key)[0]


def draw_counts(key, part):
    return block_plan(key)[1]


def level_of(key, shape, cuts, low, high):
    factor_of, own = 1.0, jax.random.fold_in(key, 6)
    for axis_at, shards_of in cuts:
        draws = jnp.exp(jax.random.uniform(jax.random.fold_in(own, axis_at), (shards_of,), jnp.float32, low / len(cuts), high / len(cuts)))
        factor_of = factor_of * jnp.repeat(draws, shape[axis_at] // shards_of).reshape([-1 if axis == axis_at else 1 for axis in range(len(shape))])
    return factor_of


def centred(rng, dims, spread, reach, pieces=(), held_as=jnp.bfloat16):
    loudness = level_of(rng, dims, pieces, -0.22, 0.18) if pieces else 1.0
    array = jax.random.normal(rng, dims, jnp.float32) * spread * loudness
    return jnp.minimum(jnp.maximum(array, -reach), reach).astype(held_as)


def setup_inputs(seed: int = 0) -> dict:
    seeds = jax.random.split(jax.random.key(seed), 6)
    return {
        "tokens": centred(seeds[0], (SEQS, LEN, D), 1.0, 6.0, ((0, 4), (1, 32))),
        "queries": draw_queries(jax.random.fold_in(seeds[5], 71), 0),
        "kv_weight": centred(seeds[2], (D, 2 * KVH * DH), D ** -0.5, 0.0625, ((1, 4),)),
        "block_list": draw_block_list(jax.random.fold_in(seeds[5], 71), 0),
        "counts": draw_counts(jax.random.fold_in(seeds[5], 71), 0),
    }


def attend_group(operands):
    query_group, keyval_group, picked, live_count = operands
    blocks = LEN // BLK
    query_blocks = query_group.reshape(blocks, BLK, HQ // KVH, DH).astype(jnp.float32)
    keyval_blocks = keyval_group.reshape(blocks, BLK, 2 * DH)
    chosen = keyval_blocks[picked].astype(jnp.float32).reshape(blocks, MAXK * BLK, 2 * DH)
    key_rows = chosen[:, :, :DH]
    value_rows = chosen[:, :, DH:]
    scores = jnp.einsum("nqhd,nkd->nqhk", query_blocks, key_rows) * (DH ** -0.5)
    slot_index = jnp.arange(MAXK * BLK) // BLK
    live_slot = slot_index[None, :] < live_count[:, None]
    scores = jnp.where(live_slot[:, None, None, :], scores, -jnp.inf)
    row_top = jnp.max(scores, axis=3, keepdims=True)
    weights = jnp.exp(scores - row_top)
    row_total = jnp.sum(weights, axis=3)
    rounded = lax.optimization_barrier(weights.astype(jnp.bfloat16)).astype(jnp.float32)
    weighted = jnp.einsum("nqhk,nkd->nqhd", rounded, value_rows)
    result = (weighted / row_total[..., None]).astype(jnp.bfloat16)
    return result.reshape(LEN, HQ // KVH, DH)


def reference(tokens, queries, kv_weight, block_list, counts):
    outputs = []
    for seq_index in range(SEQS):
        keyvals = jnp.dot(tokens[seq_index], kv_weight, preferred_element_type=jnp.float32).astype(jnp.bfloat16)
        query_group = queries[seq_index].reshape(LEN, KVH, HQ // KVH, DH).transpose(1, 0, 2, 3)
        keyval_group = keyvals.reshape(LEN, KVH, 2 * DH).transpose(1, 0, 2)
        attended = lax.map(attend_group, (query_group, keyval_group, block_list, counts))
        outputs.append(attended.transpose(1, 0, 2, 3).reshape(LEN, HQ * DH))
    return jnp.stack(outputs)
```

```python
import functools

import jax
import jax.numpy as jnp
from jax import lax
from jax.experimental import pallas as pl
from jax.experimental.pallas import tpu as pltpu
from jax.sharding import Mesh
from jax.sharding import PartitionSpec as P

HQ = 64
KVH = 8
DH = 128
BLK = 128
MAXK = 8
GROUP = HQ // KVH
PAIR = 2 * DH
ROWS = GROUP * BLK
NEG = -1e30


def attend_kernel(meta, lists, counts, q_own, q_par, kv, o_own, o_par, s_buf, p_buf, v_buf):
    step = pl.program_id(0)
    group = meta[0]
    block = meta[1] + lax.rem(meta[2] * 2 + step, 4)
    live = counts[group, block]
    scale = DH ** (-0.5)

    def run(q_ref, o_ref):
        q = q_ref[...].reshape(BLK, GROUP * DH)
        q_all = jnp.concatenate([q[:, h * DH : (h + 1) * DH] for h in range(GROUP)], axis=0)
        top = jnp.full((ROWS, DH), NEG, jnp.float32)
        for j in range(MAXK):
            start = pl.multiple_of(lists[group, block, j] * BLK, BLK)
            k_rows = kv[pl.ds(start, BLK), :DH]
            v_buf[pl.ds(j * BLK, BLK), :DH] = kv[pl.ds(start, BLK), DH:]
            scores = lax.dot_general(
                q_all, k_rows, (((1,), (1,)), ((), ())), preferred_element_type=jnp.float32
            )
            scores = jnp.where(j < live, scores * scale, NEG)
            s_buf[:, j * BLK : (j + 1) * BLK] = scores
            top = jnp.maximum(top, scores)
        row_top = jnp.max(top, axis=1, keepdims=True)
        for j in range(MAXK):
            weights = jnp.exp(s_buf[:, j * BLK : (j + 1) * BLK] - row_top)
            p_buf[:, j * BLK : (j + 1) * BLK] = weights.astype(jnp.bfloat16)
        mixed = jnp.dot(p_buf[...], v_buf[...], preferred_element_type=jnp.float32)
        out = (mixed[:, :DH] / mixed[:, DH:]).astype(jnp.bfloat16)
        for h in range(GROUP):
            o_ref[:, h * DH : (h + 1) * DH] = out[h * BLK : (h + 1) * BLK, :]

    v_buf[:, DH:] = jnp.ones((MAXK * BLK, DH), jnp.bfloat16)

    @pl.when(step < 2)
    def _():
        run(q_own, o_own)

    @pl.when(step >= 2)
    def _():
        run(q_par, o_par)


def attend(meta, lists, counts, q_own, q_par, kv):
    cols = GROUP * DH
    first = lambda s: jnp.minimum(s, 1)
    second = lambda s: jnp.maximum(s - 2, 0)
    return pl.pallas_call(
        attend_kernel,
        out_shape=(
            jax.ShapeDtypeStruct((2 * BLK, cols), jnp.bfloat16),
            jax.ShapeDtypeStruct((2 * BLK, cols), jnp.bfloat16),
        ),
        grid_spec=pltpu.PrefetchScalarGridSpec(
            num_scalar_prefetch=3,
            grid=(4,),
            in_specs=[
                pl.BlockSpec((BLK, cols), lambda s, m, l, n: (first(s), m[0])),
                pl.BlockSpec((BLK, cols), lambda s, m, l, n: (second(s), m[0] // 2)),
                pl.BlockSpec(kv.shape, lambda s, m, l, n: (0, 0), pipeline_mode=pl.Buffered(1)),
            ],
            out_specs=[
                pl.BlockSpec((BLK, cols), lambda s, m, l, n: (first(s), 0)),
                pl.BlockSpec((BLK, cols), lambda s, m, l, n: (second(s), 0)),
            ],
            scratch_shapes=[
                pltpu.VMEM((ROWS, MAXK * BLK), jnp.float32),
                pltpu.VMEM((ROWS, MAXK * BLK), jnp.bfloat16),
                pltpu.VMEM((MAXK * BLK, PAIR), jnp.bfloat16),
            ],
        ),
        compiler_params=pltpu.CompilerParams(vmem_limit_bytes=40 << 20),
        cost_estimate=pl.CostEstimate(
            flops=4 * 4 * ROWS * MAXK * BLK * DH,
            bytes_accessed=8 << 20,
            transcendentals=4 * ROWS * MAXK * BLK,
        ),
        name="attend",
    )(meta, lists, counts, q_own, q_par, kv)


def on_device(tokens, queries, kv_weight, block_list, counts):
    tokens = tokens[0]
    queries = queries[0]
    depth = kv_weight.shape[0]
    cols = GROUP * DH
    core = lax.axis_index("c")
    y = lax.axis_index("y")
    n_z = lax.axis_size("z")
    plane = lax.axis_size("x") * n_z
    n_y = lax.axis_size("y")
    place = lax.axis_index("x") * n_z + lax.axis_index("z")
    swap = [(0, 1), (1, 0)]
    around = lambda k: [(i, (i + k) % n_y) for i in range(n_y)]

    w_own = lax.dynamic_slice_in_dim(kv_weight, core * PAIR, PAIR, 1)
    part = depth // plane
    far_slice = lax.ppermute(lax.dynamic_slice_in_dim(w_own, place * part, part, 0), "y", around(2))
    tok_par = lax.ppermute(tokens, "c", swap)
    w_k, w_v = w_own[:, :DH], w_own[:, DH:]
    up_k = lax.ppermute(w_k, "y", around(-1))
    down_k = lax.ppermute(w_k, "y", around(1))
    up_v = lax.ppermute(w_v, "y", around(-1))
    down_v = lax.ppermute(w_v, "y", around(1))
    q_view = queries.reshape(2 * BLK, n_y, 2, cols)
    q_send = lax.dynamic_index_in_dim(q_view, 1 - core, 2, keepdims=False).reshape(2 * BLK, n_y * cols)
    q_par = lax.ppermute(q_send, "c", swap)

    def project(weight):
        own = jnp.dot(tokens, weight, preferred_element_type=jnp.float32).astype(jnp.bfloat16)
        par = jnp.dot(tok_par, weight, preferred_element_type=jnp.float32).astype(jnp.bfloat16)
        return jnp.where(core == 0, jnp.concatenate([own, par]), jnp.concatenate([par, own]))

    def spread(rows):
        return lax.all_gather(rows, ("x", "z"), axis=0, tiled=True)

    far = spread(far_slice)
    kv_own = spread(project(w_own))
    kv_k = spread(project(jnp.concatenate([up_k, down_k], axis=1)))
    kv_far = spread(project(far))
    kv_v = spread(project(jnp.concatenate([up_v, down_v], axis=1)))
    kv_up = jnp.concatenate([kv_k[:, :DH], kv_v[:, :DH]], axis=1)
    kv_down = jnp.concatenate([kv_k[:, DH:], kv_v[:, DH:]], axis=1)

    def head(step, kv):
        which = lax.rem(y + step, n_y)
        meta = jnp.stack([which * 2 + core, place * 4, core]).astype(jnp.int32)
        own, par = attend(meta, block_list, counts, queries, q_par, kv)
        return own, lax.ppermute(par, "c", swap)

    pieces = [head(0, kv_own), head(1, kv_up), head(2, kv_far), head(3, kv_down)]
    own = jnp.stack([p[0] for p in pieces])
    par = jnp.stack([p[1] for p in pieces])
    own = jnp.roll(own, y, axis=0)
    par = jnp.roll(par, y, axis=0)
    even = jnp.where(core == 0, own, par)
    odd = jnp.where(core == 0, par, own)
    out = jnp.stack([even, odd], axis=1)
    return out.transpose(2, 0, 1, 3).reshape(1, 2 * BLK, 2 * n_y * cols)


def solution(mesh):
    fine = Mesh(mesh.devices.reshape(4, 4, 2, 4), ("x", "z", "c", "y"))
    ctx = ("x", "z", "c")
    return jax.shard_map(
        on_device,
        mesh=fine,
        in_specs=(P("y", ctx, None), P("y", ctx, None), P(None, "y"), P(), P()),
        out_specs=P("y", ctx, None),
        check_vma=False,
    )
```

```python
import functools

import jax
import jax.numpy as jnp
from jax import lax
from jax.experimental import pallas as pl
from jax.experimental.pallas import tpu as pltpu
from jax.sharding import Mesh
from jax.sharding import PartitionSpec as P

HQ = 64
KVH = 8
DH = 128
BLK = 128
MAXK = 8
GROUP = HQ // KVH
PAIR = 2 * DH
COLS = GROUP * DH
ROWS = GROUP * BLK
RING = 4
HALF = 256
PIECE = 512
MESH_ID = pl.DeviceIdType.MESH
BF16 = jnp.bfloat16
OWN, FAR_W, NEAR_K, FAR, NEAR_V = range(5)
LOG2E = 1.4426950408889634


def fused_kernel(
    first, second, third, bias, tokens, queries, w, out,
    tok, q, w_own, w_nk, w_nv, g0, g1, g2, g3, g4, s_buf, p_buf, v_buf, ob,
    local_sem, far_send, far_recv, tok_send, tok_recv, q_send, q_recv,
    w_send, w_recv, ag_send, ag_recv, o_local, o_send, o_recv,
):
    g = [g0, g1, g2, g3, g4]
    x, z, c, y = (lax.axis_index(n) for n in ("x", "z", "c", "y"))
    a = x + c * (z - x)
    b = z + c * (x - z)
    mod = lambda v: lax.rem(v + RING, RING)
    ap, am, bp, bm = mod(a + 1), mod(a - 1), mod(b + 1), mod(b - 1)
    plane = lambda a_, b_: (a_ + c * (b_ - a_), b_ + c * (a_ - b_), c, y)
    to_ap, to_am, to_bp, to_bm = plane(ap, b), plane(am, b), plane(a, bp), plane(a, bm)
    up, down, far = (x, z, c, mod(y + 1)), (x, z, c, mod(y - 1)), (x, z, c, mod(y + 2))
    mate = (x, z, 1 - c, y)
    everyone = [to_ap, to_am, to_bp, to_bm, up, down, far, mate]
    my_cols = pl.multiple_of(c * PAIR, PAIR)
    q_col = lambda h, core: pl.ds(pl.multiple_of((mod(y + h) * 2 + core) * COLS, COLS), COLS)

    def remote(src, dst, send, recv, dev):
        return pltpu.make_async_remote_copy(
            src_ref=src, dst_ref=dst, send_sem=send, recv_sem=recv,
            device_id=dev, device_id_type=MESH_ID,
        )

    own_copies = [
        pltpu.make_async_copy(tokens, tok.at[c], local_sem.at[0]),
        pltpu.make_async_copy(w.at[:, :, pl.ds(my_cols, PAIR)], w_own, local_sem.at[1]),
    ]
    q_copies = [
        pltpu.make_async_copy(queries.at[:, q_col(h, c)], q.at[h, c], local_sem.at[2 + h])
        for h in range(RING)
    ]
    for copy in own_copies + q_copies:
        copy.start()
    v_buf[:, DH:] = jnp.ones((MAXK * BLK, DH), BF16)

    barrier = pltpu.get_barrier_semaphore()
    for dev in everyone:
        pl.semaphore_signal(barrier, inc=1, device_id=dev, device_id_type=MESH_ID)
    pl.semaphore_wait(barrier, len(everyone))

    far_copy = remote(
        w.at[pl.ds((a * RING + b) * RING, RING), :, pl.ds(my_cols, PAIR)], g[FAR_W].at[a, b], far_send, far_recv, far
    )
    tok_copy = remote(tokens, tok.at[c], tok_send, tok_recv, mate)
    k_cols = w.at[:, :, pl.ds(my_cols, DH)]
    v_cols = w.at[:, :, pl.ds(pl.multiple_of(my_cols + DH, DH), DH)]
    w_copies = [
        remote(k_cols, w_nk.at[:, :, DH:], w_send.at[0], w_recv.at[0], up),
        remote(k_cols, w_nk.at[:, :, :DH], w_send.at[1], w_recv.at[1], down),
        remote(v_cols, w_nv.at[:, :, DH:], w_send.at[2], w_recv.at[2], up),
        remote(v_cols, w_nv.at[:, :, :DH], w_send.at[3], w_recv.at[3], down),
    ]
    q_moves = [
        remote(queries.at[:, q_col(h, 1 - c)], q.at[h, c], q_send.at[h], q_recv.at[h], mate)
        for h in range(RING)
    ]
    for copy in [far_copy, tok_copy] + w_copies + q_moves:
        copy.start()

    def move(u, k):
        src, dev = [
            (g[u].at[a, b], to_ap),
            (g[u].at[a, b], to_am),
            (g[u].at[am, b, pl.ds(0, 2)], to_ap),
            (g[u].at[ap, b, pl.ds(2, 2)], to_am),
            (g[u].at[:, b], to_bp),
            (g[u].at[:, b], to_bm),
            (g[u].at[:, bm, pl.ds(0, 2)], to_bp),
            (g[u].at[:, bp, pl.ds(2, 2)], to_bm),
        ][k]
        return remote(src, src, ag_send.at[u, k], ag_recv.at[u, k], dev)

    def s0(u):
        move(u, 0).start()
        move(u, 1).start()

    def s1(u):
        move(u, 0).wait_recv()
        move(u, 2).start()
        move(u, 1).wait_recv()
        move(u, 3).start()

    def s2(u):
        move(u, 2).wait_recv()
        move(u, 3).wait_recv()
        move(u, 4).start()
        move(u, 5).start()

    def s3(u):
        move(u, 4).wait_recv()
        move(u, 6).start()
        move(u, 5).wait_recv()
        move(u, 7).start()

    def s4(u):
        move(u, 6).wait_recv()
        move(u, 7).wait_recv()

    def project(u, owner, weight):
        rows = jnp.dot(tok[owner], weight[...].reshape(-1, PAIR), preferred_element_type=jnp.float32)
        g[u][a, b, pl.ds(owner * 2, 2)] = rows.astype(BF16).reshape(2, BLK, PAIR)

    def project_both(u, weight):
        @pl.loop(0, 2)
        def _(i):
            project(u, i, weight)

    sources = [
        (OWN, 0, OWN, DH),
        (NEAR_K, 0, NEAR_V, 0),
        (FAR, 0, FAR, DH),
        (NEAR_K, DH, NEAR_V, DH),
    ]

    def attend(h, mine, i):
        owner = c if mine else 1 - c
        group = mod(y + h) * 2 + c
        block = (x * RING + z) * 4 + owner * 2 + i
        entry = (group * 64 + block) * MAXK
        ku, kc, vu, vc = sources[h]
        q_rows = q[h, owner, pl.ds(pl.multiple_of(i * BLK, BLK), BLK), :]
        q_all = jnp.concatenate([q_rows[:, n * DH : (n + 1) * DH] for n in range(GROUP)], axis=0)
        top = None
        for j in range(MAXK):
            ka, kbb, kr = first[entry + j], second[entry + j], third[entry + j]
            k_rows = g[ku][ka, kbb, kr, :, kc : kc + DH]
            v_rows = g[vu][ka, kbb, kr, :, vc : vc + DH]
            v_buf[j * BLK : (j + 1) * BLK, :DH] = v_rows
            scores = lax.dot_general(
                q_all, k_rows, (((1,), (1,)), ((), ())), preferred_element_type=jnp.float32
            )
            if j >= 4:
                scores = scores + bias[entry + j]
            s_buf[:, j * BLK : (j + 1) * BLK] = scores
            top = scores if top is None else jnp.maximum(top, scores)
        row_top = jnp.max(top, axis=1, keepdims=True)
        for j in range(MAXK):
            weights = jnp.exp2((s_buf[:, j * BLK : (j + 1) * BLK] - row_top) * (DH ** (-0.5) * LOG2E))
            p_buf[:, j * BLK : (j + 1) * BLK] = weights.astype(BF16)
        mixed = jnp.dot(p_buf[...], v_buf[...], preferred_element_type=jnp.float32)
        res = (mixed[:, :DH] / mixed[:, DH:]).astype(BF16)
        slot = (0 if mine else 2) + i
        for n in range(GROUP):
            ob[h, slot, :, n * DH : (n + 1) * DH] = res[n * BLK : (n + 1) * BLK, :]

    def result(h, mine, i):
        at = out.at[pl.ds(pl.multiple_of(i * BLK, BLK), BLK), q_col(h, c)]
        if mine:
            return pltpu.make_async_copy(ob.at[h, i], at, o_local.at[h, i])
        return remote(ob.at[h, 2 + i], at, o_send.at[h, i], o_recv.at[h, i], mate)

    def head(h, mine):
        @pl.loop(0, 2)
        def _(i):
            attend(h, mine, i)
            result(h, mine, i).start()

    for copy in own_copies:
        copy.wait()
    project(OWN, c, w_own)
    far_copy.wait_recv()
    s0(FAR_W)
    tok_copy.wait_recv()
    project(OWN, 1 - c, w_own)
    s0(OWN)
    s1(FAR_W)
    s1(OWN)
    s2(FAR_W)
    s2(OWN)
    s3(FAR_W)
    s3(OWN)
    s4(FAR_W)
    project_both(FAR, g[FAR_W])
    s0(FAR)
    s4(OWN)
    w_copies[0].wait_recv()
    w_copies[1].wait_recv()
    project_both(NEAR_K, w_nk)
    s0(NEAR_K)
    s1(FAR)
    s1(NEAR_K)
    s2(FAR)
    for copy in q_copies:
        copy.wait()
    for copy in q_moves:
        copy.wait_recv()
    head(0, False)
    s2(NEAR_K)
    s3(FAR)
    head(0, True)
    s4(FAR)
    s3(NEAR_K)
    head(2, False)
    s4(NEAR_K)
    w_copies[2].wait_recv()
    w_copies[3].wait_recv()
    project_both(NEAR_V, w_nv)
    s0(NEAR_V)
    s1(NEAR_V)
    s2(NEAR_V)
    head(2, True)
    s3(NEAR_V)
    s4(NEAR_V)
    head(1, False)
    head(3, False)
    head(1, True)
    head(3, True)

    far_copy.wait_send()
    tok_copy.wait_send()
    for copy in w_copies + q_moves:
        copy.wait_send()
    for u in range(5):
        for k in range(8):
            move(u, k).wait_send()
    for h in range(RING):
        for i in range(2):
            result(h, True, i).wait()
            result(h, False, i).wait()


def fused(tables, bias, tokens, queries, w):
    dma = pltpu.SemaphoreType.DMA
    anywhere = pl.BlockSpec(memory_space=pl.ANY)
    smem = pl.BlockSpec(memory_space=pltpu.SMEM)
    rows, depth = tokens.shape
    return pl.pallas_call(
        fused_kernel,
        out_shape=jax.ShapeDtypeStruct(queries.shape, BF16),
        in_specs=[smem, smem, smem, smem, anywhere, anywhere, anywhere],
        out_specs=anywhere,
        scratch_shapes=[
            pltpu.VMEM((2, rows, depth), BF16),
            pltpu.VMEM((RING, 2, rows, COLS), BF16),
            pltpu.VMEM((depth // BLK, BLK, PAIR), BF16),
            pltpu.VMEM((depth // BLK, BLK, PAIR), BF16),
            pltpu.VMEM((depth // BLK, BLK, PAIR), BF16),
            *[pltpu.VMEM((RING, RING, RING, BLK, PAIR), BF16) for _ in range(5)],
            pltpu.VMEM((ROWS, MAXK * BLK), jnp.float32),
            pltpu.VMEM((ROWS, MAXK * BLK), BF16),
            pltpu.VMEM((MAXK * BLK, PAIR), BF16),
            pltpu.VMEM((RING, 4, BLK, COLS), BF16),
            dma((6,)), dma, dma, dma, dma, dma((4,)), dma((4,)),
            dma((4,)), dma((4,)), dma((5, 8)), dma((5, 8)),
            dma((RING, 2)), dma((RING, 2)), dma((RING, 2)),
        ],
        compiler_params=pltpu.CompilerParams(
            collective_id=0, has_side_effects=True, vmem_limit_bytes=67043328
        ),
        name="fused",
    )(*tables, bias, tokens, queries, w)


def on_device(tokens, queries, kv_weight, block_list, counts):
    c = lax.axis_index("c")
    chip, row = block_list // 4, block_list % 4
    kx, kz = chip // RING, chip % RING
    tables = (jnp.where(c == 0, kx, kz), jnp.where(c == 0, kz, kx), row)
    bias = jnp.where(jnp.arange(MAXK) < counts[..., None], 0.0, -1e30).astype(jnp.float32)
    weight = kv_weight.reshape(-1, BLK, kv_weight.shape[1])
    tables = tuple(t.reshape(-1) for t in tables)
    return fused(tables, bias.reshape(-1), tokens[0], queries[0], weight)[None]


def solution(mesh):
    fine = Mesh(mesh.devices.reshape(4, 4, 2, 4), ("x", "z", "c", "y"))
    ctx = ("x", "z", "c")
    return jax.shard_map(
        on_device,
        mesh=fine,
        in_specs=(P("y", ctx, None), P("y", ctx, None), P(None, "y"), P(), P()),
        out_specs=P("y", ctx, None),
        check_vma=False,
    )
```
